32 devices in a mesh: rows: 8 (over z, y), feat: 4 (over x, core).
Axes of the slice: x: 2, y: 2, z: 4, core: 2. Of those that a mesh axis runs over, the one named last changes fastest.
Arguments:
- features: bfloat16 [8192, 64], P('rows', 'feat'), may hold values from -0.75 to 0.75
- probes: bfloat16 [8192, 32], P('rows', 'feat'), may hold values from -6 to 6
- theta: float32 [1], replicated, may hold values from 0.18 to 0.69
- block_mask: int32 [8, 9], P('rows'), may hold values 0 or 1
- order: int32 [8, 1024], P('rows'), may hold values from 0 to 1023, each once within a row
Outputs:
- kernel_probes: float32 [8192, 32], P('rows', 'feat')
- deriv_probes: float32 [8192, 32], P('rows', 'feat')
The draws below stay inside these ranges and needn't reach their ends.
All inputs are finite; a program needn't handle non-finite values. No bound on the sum of `block_mask` on one device may be relied on, other than what follows from the above.
Results may differ from the reference program's by a relative error of at most 0.003.
Values may be sent and summed in bfloat16 or wider, within the bound.
No kernel may reach another device: no remote copies, remote signals or barrier semaphores. Data moves between devices by JAX's collectives and lax.ppermute only.
A program may use at most 64 MiB of HBM per device.

```python
import jax
import jax.numpy as jnp
from jax import lax

F = 64
P_SIZE = 32
ROWS_DEV = 1024
NBLK = 8
N = 8192


def touch_ends(entries, rng, smallest, top_value):
    longest = entries.shape.index(max(entries.shape))
    spots = []
    for shift in (0, 1):
        where = [jax.random.randint(jax.random.fold_in(rng, axis), (), 0, length) for axis, length in enumerate(entries.shape)]
        where[longest] = (where[longest] + shift) % entries.shape[longest]
        spots.append(tuple(where))
    return entries.at[spots[0]].set(smallest).at[spots[1]].set(top_value)


def levels(rng, dims, cuts, low, largest):
    def one(position, shards_of):
        heights = jax.random.uniform(jax.random.fold_in(jax.random.fold_in(rng, 6), position), (shards_of,), jnp.float32, low / len(cuts), largest / len(cuts))
        return jnp.repeat(jnp.exp(heights), dims[position] // shards_of).reshape((-1,) + (1,) * (len(dims) - position - 1))

    factor_of = one(*cuts[0])
    for cut in cuts[1:]:
        factor_of = factor_of * one(*cut)
    return factor_of


def gaussian(stream_key, extent, deviation, most, pieces=(), held_as=jnp.bfloat16):
    entries = deviation * jax.random.normal(stream_key, extent, jnp.float32)
    if pieces:
        entries = entries * levels(stream_key, extent, pieces, -0.22, 0.18)
    return jnp.clip(entries, -most, most).astype(held_as)


def setup_inputs(seed: int = 0) -> dict:
    streams_of = jax.random.split(jax.random.key(seed), 6)
    features = gaussian(streams_of[0], (N, F), (1.0 / F ** 0.5), 0.75, ((0, 8), (1, 4)))
    probes = gaussian(streams_of[1], (N, P_SIZE), 1.0, 6.0, ((0, 8), (1, 4)))
    theta = jnp.clip(jax.random.uniform(streams_of[2], (1,), jnp.float32, 0.18, 0.69), 0.18, 0.69)
    block_mask = touch_ends((jax.random.randint(streams_of[3], (NBLK, 9), 0, 4) < 3).astype(jnp.int32), jax.random.fold_in(streams_of[3], 1), 0, 1)
    order = jax.vmap(lambda own: jax.random.permutation(own, ROWS_DEV))(jax.random.split(streams_of[4], NBLK)).reshape((NBLK, ROWS_DEV)).astype(jnp.int32)
    return {"features": features, "probes": probes, "theta": theta, "block_mask": block_mask, "order": order}


def reference(features, probes, theta, block_mask, order):
    feats = features.reshape(NBLK, ROWS_DEV, F)
    raw = probes.reshape(NBLK, ROWS_DEV, P_SIZE)
    ordered = jnp.take_along_axis(raw, order.astype(jnp.int32)[:, :, None], axis=1)
    squares = lax.optimization_barrier(jnp.sum(feats.astype(jnp.float32) ** 2, axis=2))
    scale = jnp.exp(-2.0 * theta[0])

    def one_block(index):
        rows_f = lax.dynamic_index_in_dim(feats, index, 0, keepdims=False)
        rows_sq = lax.dynamic_index_in_dim(squares, index, 0, keepdims=False)
        total_k = jnp.zeros((ROWS_DEV, P_SIZE), jnp.float32)
        total_d = jnp.zeros((ROWS_DEV, P_SIZE), jnp.float32)
        for offset in range(9):
            other = ((index + offset - 4) % NBLK).astype(jnp.int32)
            cols_f = lax.dynamic_index_in_dim(feats, other, 0, keepdims=False)
            cols_sq = lax.dynamic_index_in_dim(squares, other, 0, keepdims=False)
            cols_z = lax.dynamic_index_in_dim(ordered, other, 0, keepdims=False)
            cross = lax.dot_general(rows_f, cols_f, (((1,), (1,)), ((), ())), preferred_element_type=jnp.float32)
            dist2 = jnp.maximum(rows_sq[:, None] + cols_sq[None, :] - 2.0 * cross, 0.0)
            radius2 = dist2 * scale
            radius = jnp.sqrt(radius2)
            inside = jnp.maximum(1.0 - radius, 0.0)
            inside2 = inside * inside
            kern = (inside2 * inside2 * (4.0 * radius + 1.0)).astype(jnp.bfloat16)
            deriv = (20.0 * radius2 * inside2 * inside).astype(jnp.bfloat16)
            term_k = jnp.dot(kern, cols_z, preferred_element_type=jnp.float32)
            term_d = jnp.dot(deriv, cols_z, preferred_element_type=jnp.float32)
            if offset == 4:
                total_k = total_k + term_k
                total_d = total_d + term_d
            else:
                active = block_mask[index, offset] > 0
                total_k = total_k + jnp.where(active, term_k, 0.0)
                total_d = total_d + jnp.where(active, term_d, 0.0)
        return (total_k, total_d)
    out_k, out_d = lax.map(one_block, jnp.arange(NBLK, dtype=jnp.int32))
    return (out_k.reshape(N, P_SIZE), out_d.reshape(N, P_SIZE))
```

```python
import functools

import jax
import jax.numpy as jnp
from jax import lax
from jax.experimental import pallas as pl
from jax.experimental.pallas import tpu as pltpu
from jax.sharding import PartitionSpec as P

TINY = 1e-30
LIMIT = 12 << 20
PAD = 16
VMEM = pl.BlockSpec(memory_space=pltpu.VMEM)
SMEM = pl.BlockSpec(memory_space=pltpu.SMEM)


def shifted(value, axis, steps):
    count = lax.axis_size(axis)
    return lax.ppermute(value, axis, [(i, (i + steps) % count) for i in range(count)])


def swapped(value, axis, bits):
    count = lax.axis_size(axis)
    return lax.ppermute(value, axis, [(i, i ^ bits) for i in range(count)])


def bit_order(count):
    width = count.bit_length() - 1
    return [int(format(j, f"0{width}b")[::-1], 2) if width else 0 for j in range(count)]


def split3(value):
    high = value.astype(jnp.bfloat16)
    rest = value - high.astype(jnp.float32)
    middle = rest.astype(jnp.bfloat16)
    low = (rest - middle.astype(jnp.float32)).astype(jnp.bfloat16)
    return high, middle, low


def norm_rows(parts, first):
    columns = parts[0].shape[1]
    row = lax.broadcasted_iota(jnp.int32, (PAD, columns), 0)
    ones = 3 - first
    out = jnp.where((row >= ones) & (row < ones + 3), 1.0, 0.0)
    for i, part in enumerate(parts):
        out = jnp.where(row == first + i, part.astype(jnp.float32), out)
    return out.astype(jnp.bfloat16)


def scale_row(theta_ref, columns):
    return jnp.exp(jnp.full((1, columns), -2.0 * theta_ref[0], jnp.float32))


def prep_kernel(widths, theta_ref, order_ref, *refs):
    feats_n, probes_n = widths
    pieces, (own_ref, send_ref) = refs[:-2], refs[-2:]
    step = feats_n + probes_n
    rows = order_ref.shape[1]
    quarter = send_ref.shape[1]
    start = pl.multiple_of(lax.axis_index("feat") * quarter, quarter)
    slots = [(ref, i * step) for ref in pieces for i in range(ref.shape[0] // step)]
    feats = jnp.concatenate([ref[at : at + feats_n, :] for ref, at in slots], axis=0)
    total = feats.shape[0]
    wide = feats.astype(jnp.float32)
    scale = scale_row(theta_ref, rows)
    norms = jnp.sum(wide * wide, axis=0, keepdims=True) * scale
    for i, part in enumerate(split3(wide * (-2.0 * scale))):
        own_ref[i * total : (i + 1) * total, :] = part
    own_ref[3 * total :, :] = norm_rows(split3(norms), 0)
    for j, (ref, at) in enumerate(slots):
        send_ref[j * feats_n : (j + 1) * feats_n, :] = ref[at : at + feats_n, pl.ds(start, quarter)]
    order = order_ref[:, pl.ds(start, quarter)]
    source = lax.broadcasted_iota(jnp.int32, (rows, quarter), 0)
    pick = jnp.where(source == order, 1.0, 0.0).astype(jnp.bfloat16)
    raw = jnp.concatenate(
        [slots[j][0][slots[j][1] + feats_n : slots[j][1] + step, :] for j in bit_order(len(slots))], axis=0
    )
    picked = jnp.dot(raw, pick, preferred_element_type=jnp.float32)
    send_ref[total:, :] = picked.astype(jnp.bfloat16)


def prep(widths, theta, order, pieces):
    count = sum(p.shape[0] for p in pieces) // sum(widths)
    rows = order.shape[1]
    return pl.pallas_call(
        functools.partial(prep_kernel, widths),
        out_shape=(
            jax.ShapeDtypeStruct((3 * count * widths[0] + PAD, rows), jnp.bfloat16),
            jax.ShapeDtypeStruct((count * sum(widths), rows // count), jnp.bfloat16),
        ),
        in_specs=[SMEM, VMEM] + [VMEM] * len(pieces),
        out_specs=(VMEM, VMEM),
        compiler_params=pltpu.CompilerParams(vmem_limit_bytes=LIMIT),
        cost_estimate=pl.CostEstimate(flops=1 << 25, bytes_accessed=1 << 20, transcendentals=0),
        name="prep",
    )(theta, order, *pieces)


def tile_kernel(plan, has_acc, last, theta_ref, mask_ref, own_ref, *refs):
    panels, rest = refs[: len(plan)], refs[len(plan) :]
    acc_ref = rest[0] if has_acc else None
    outs = rest[1:] if has_acc else rest
    rows = own_ref.shape[1]
    total = (own_ref.shape[0] - PAD) // 3
    count = lax.axis_size("rows")
    me = lax.axis_index("rows")
    acc = outs[0] if not last else outs[-1]
    started = False
    for ref, offsets in zip(panels, plan, strict=True):
        height = ref.shape[0] // len(offsets)
        quarter = ref.shape[1]
        for i, offset in enumerate(offsets):
            base = i * height
            kind, amount = offset
            if kind == "shift":
                weight = mask_ref[0, 4 + amount] if amount else jnp.int32(1)
                weight = jnp.where(weight > 0, 1.0, 0.0)
            elif amount == 0:
                weight = jnp.float32(1.0)
            else:
                gap = lax.rem((me ^ amount) - me + 4 + 2 * count, count)
                weight = jnp.where(mask_ref[0, gap] > 0, 1.0, 0.0)
                again = jnp.where(mask_ref[0, 8] > 0, 1.0, 0.0)
                weight = weight + jnp.where(gap == 0, again, 0.0)
            feats = ref[base : base + total, :]
            wide = feats.astype(jnp.float32)
            norms = jnp.sum(wide * wide, axis=0, keepdims=True) * scale_row(theta_ref, quarter)
            extended = jnp.concatenate([feats, feats, feats, norm_rows(split3(norms), 3)], axis=0)
            probes = ref[base + total : base + height, :].astype(jnp.float32) * weight
            probes_k = (probes * 4.0).astype(jnp.bfloat16)
            probes_d = probes.astype(jnp.bfloat16)
            half = probes.shape[0]
            for at in range(0, rows, 256):
                here = slice(at, at + 256)
                raw = lax.dot_general(
                    extended, own_ref[:, here], (((0,), (0,)), ((), ())), preferred_element_type=jnp.float32
                )
                radius2 = jnp.maximum(raw, TINY)
                radius = radius2 * lax.rsqrt(radius2)
                inside = jnp.maximum(1.0 - radius, 0.0)
                inside3 = inside * inside * inside
                kern = (inside3 * (inside * (radius + 0.25))).astype(jnp.bfloat16)
                deriv = (inside3 * (radius2 * 20.0)).astype(jnp.bfloat16)
                first = jnp.dot(probes_k, kern, preferred_element_type=jnp.float32)
                second = jnp.dot(probes_d, deriv, preferred_element_type=jnp.float32)
                if not started and has_acc:
                    acc[:half, here] = acc_ref[:half, here] + first
                    acc[half:, here] = acc_ref[half:, here] + second
                elif not started:
                    acc[:half, here] = first
                    acc[half:, here] = second
                else:
                    acc[:half, here] += first
                    acc[half:, here] += second
            started = True
    if last:
        keep_ref, send_ref, _ = outs
        half = acc.shape[0] // 2
        part = half // 2
        for k in range(2):
            keep_ref[k * part : (k + 1) * part, :] = acc[k * half : k * half + part, :]
            send_ref[k * part : (k + 1) * part, :] = acc[k * half + part : (k + 1) * half, :].astype(send_ref.dtype)


def tiles(theta, mask, own, panels, plan, acc, last):
    rows = own.shape[1]
    total = (own.shape[0] - PAD) // 3
    height = panels[0].shape[0] // len(plan[0])
    out_rows = 2 * (height - total)
    scratch = []
    if last:
        shape = (out_rows // 2, rows)
        out_shape = (jax.ShapeDtypeStruct(shape, jnp.float32), jax.ShapeDtypeStruct(shape, jnp.bfloat16))
        scratch = [pltpu.VMEM((out_rows, rows), jnp.float32)]
    else:
        out_shape = jax.ShapeDtypeStruct((out_rows, rows), jnp.float32)
    operands = [theta, mask, own, *panels] + ([acc] if acc is not None else [])
    count = sum(len(p) for p in plan)
    return pl.pallas_call(
        functools.partial(tile_kernel, plan, acc is not None, last),
        out_shape=out_shape,
        in_specs=[SMEM, SMEM] + [VMEM] * (len(operands) - 2),
        out_specs=(VMEM, VMEM) if last else VMEM,
        scratch_shapes=scratch,
        compiler_params=pltpu.CompilerParams(vmem_limit_bytes=LIMIT),
        cost_estimate=pl.CostEstimate(flops=count << 29, bytes_accessed=1 << 20, transcendentals=0),
        name=f"tiles{count}",
    )(*operands)


def body(features, probes, theta, block_mask, order):
    group = lax.axis_size("feat")
    count = lax.axis_size("rows")
    widths = (features.shape[1], probes.shape[1])
    stages = [1 << i for i in range(group.bit_length() - 1)]

    held = jnp.concatenate([features.T, probes.T], axis=0)
    pieces = [held]
    for bits in stages:
        held = pieces[0] if len(pieces) == 1 else jnp.concatenate(pieces, axis=0)
        pieces = [held, swapped(held, "feat", bits)]
    own, mine = prep(widths, theta, order, pieces)

    call = functools.partial(tiles, theta, block_mask, own)
    if count == 8:
        near = {k: swapped(mine, "rows", k) for k in (6, 4, 2)}
        first = jnp.concatenate([mine, near[2]], axis=0)
        second = jnp.concatenate([near[4], near[6]], axis=0)
        first_y = swapped(first, "rows", 1)
        second_y = swapped(second, "rows", 1)
        acc = call([mine], [[("xor", 0)]], None, False)
        acc = call([near[2], near[4], near[6]], [[("xor", 2)], [("xor", 4)], [("xor", 6)]], acc, False)
        acc = call([first_y], [[("xor", 1), ("xor", 3)]], acc, False)
        keep, send = call([second_y], [[("xor", 5), ("xor", 7)]], acc, True)
    else:
        acc = call([mine], [[("shift", 0)]], None, False)
        for step in range(1, 5):
            pair = [shifted(mine, "rows", -step), shifted(mine, "rows", step)]
            acc = call(pair, [[("shift", step)], [("shift", -step)]], acc, step == 4)
        keep, send = acc

    for bits in stages:
        summed = keep + swapped(send, "feat", bits).astype(jnp.float32)
        if bits == stages[-1]:
            break
        half = summed.shape[0] // 2
        part = half // 2
        keep = jnp.concatenate([summed[:part], summed[half : half + part]], axis=0)
        send = jnp.concatenate([summed[part:half], summed[half + part :]], axis=0).astype(jnp.bfloat16)
    out = summed.shape[0] // 2
    return (summed[:out].T, summed[out:].T)


def solution(mesh):
    return jax.shard_map(
        body,
        mesh=mesh,
        in_specs=(P("rows", "feat"), P("rows", "feat"), P(), P("rows", None), P("rows", None)),
        out_specs=(P("rows", "feat"), P("rows", "feat")),
        check_vma=False,
    )
```
